32 devices in a mesh: basin: 2 (over x), dom: 8 (over z, y), hid: 2 (over core).
Axes of the slice: x: 2, y: 2, z: 4, core: 2. Of those that a mesh axis runs over, the one named last changes fastest.
Arguments:
- feats: bfloat16 [32768, 512], P(('basin', 'dom'), 'hid'), parts along dimension 0, may hold values from -6 to 6
- tiles: bfloat16 [256, 16, 128, 128], P(('basin', 'dom')), parts along dimension 0, may hold values from -0.125 to 0.125
- tile_cols: int32 [256, 16], P(('basin', 'dom')), parts along dimension 0, may hold values from 0 to 39, as said below
- sends: int32 [16, 3, 8], P(('basin', 'dom')), parts along dimension 0, may hold values from 0 to 15, as said below
- pins: int32 [16, 32], P(('basin', 'dom')), parts along dimension 0, may hold values from 0 to 2047, as said below
- weight: bfloat16 [512, 512], P(None, 'hid'), may hold values from -0.25 to 0.25
- bias: float32 [512], P('hid'), may hold values from -3 to 3
- cotan: bfloat16 [32768, 512], P(('basin', 'dom'), 'hid'), parts along dimension 0, may hold values from -6 to 6
Outputs:
- out: bfloat16 [32768, 512], P(('basin', 'dom'), 'hid'), parts along dimension 0
- dfeat: bfloat16 [32768, 512], P(('basin', 'dom'), 'hid'), parts along dimension 0
- dweight: float32 [1024, 512], P('basin', 'hid'), parts along dimension 0
- dbias: float32 [1024], P(('basin', 'hid')), parts along dimension 0
The draws below stay inside these ranges and needn't reach their ends.
There are 2 independent parts, one for each index of `basin`. The reference program is written for one: setup_inputs(seed, part) draws one part's arguments, and reference() takes and returns one part's arrays. A program takes and returns all parts, laid end to end along the dimension named above; an argument that names none is the same for every part. Nothing has to cross between parts.
Inputs may be any that keep to these rules, and one draw needn't show every extreme that they name: `tile_cols`: every one of a partition's 40 sources is read by at least one of its tiles. `sends`: within one partition and matching the entries are distinct; every owned block of a partition is sent in some matching. `pins`: entries may repeat.
All inputs are finite; a program needn't handle non-finite values.
Results may differ from the reference program's by a relative error of at most 0.0054.
Values may be sent and summed in bfloat16 or wider, within the bound.
A program may use at most 128 MiB of HBM per device.

```python
import math
import jax
import jax.numpy as jnp
from jax import lax

H = 512
VERT_DEV = 2048
K = 16
PINS = 32
BLOCKS_DEV = 16
SEND_BLOCKS = 8
SOURCES = 40
VERTS = 16384
RBLK = 128
N_DOM = 8


def draw_tile_cols(key, part):
    slots = BLOCKS_DEV * K

    def one_part(sub):
        first, second, third = jax.random.split(sub, 3)
        base = jax.random.permutation(first, SOURCES)
        extra = jax.random.randint(second, (slots - SOURCES,), 0, SOURCES)
        return jax.random.permutation(third, jnp.concatenate([base, extra]))
    keys = jax.random.split(jax.random.fold_in(key, 11), N_DOM)
    return jax.vmap(one_part)(keys).reshape(N_DOM * BLOCKS_DEV, K).astype(jnp.int32)


def draw_sends(key, part):
    keys = jax.random.split(jax.random.fold_in(key, 3), N_DOM)
    slot = (jnp.arange(3)[:, None] * SEND_BLOCKS + jnp.arange(SEND_BLOCKS)[None, :]) % BLOCKS_DEV
    return jax.vmap(lambda sub: jax.random.permutation(sub, BLOCKS_DEV)[slot])(keys).astype(jnp.int32)


def draw_pins(key, part):
    first, second = jax.random.split(jax.random.fold_in(key, 7))
    keys = jax.random.split(first, N_DOM)
    ids = jax.vmap(lambda sub: jax.random.permutation(sub, VERT_DEV)[:PINS])(keys)
    chosen = jax.random.randint(second, (), 0, N_DOM)
    rowsel = jnp.arange(N_DOM)[:, None] == chosen
    colsel = jnp.arange(PINS)[None, :]
    ends = jnp.where(colsel == 0, 0, VERT_DEV - 1)
    fixed = rowsel & (colsel < 2)
    return jnp.where(fixed, ends, ids).astype(jnp.int32)


def level_of(key, dims, shards, low, top_value):
    level = 1.0
    for axis_at, blocks in shards:
        steps = jax.random.uniform(jax.random.fold_in(jax.random.fold_in(key, 6), axis_at), (blocks,), jnp.float32, low / len(shards), top_value / len(shards))
        level = level * jnp.repeat(jnp.exp(steps), dims[axis_at] // blocks).reshape((-1,) + (1,) * (len(dims) - 1 - axis_at))
    return level


def normal_values(own_key, dims, deviation, most, shards=(), held_as=jnp.bfloat16):
    factor_of = level_of(own_key, dims, shards, -0.22, 0.18) if shards else 1.0
    values = jax.random.normal(own_key, dims, jnp.float32) * deviation * factor_of
    return jnp.minimum(jnp.maximum(values, -most), most).astype(held_as)


def setup_inputs(seed: int = 0, part: int = 0) -> dict:
    arg_keys = jax.random.split(jax.random.key(seed), 9)
    part_splits = jax.random.split(jax.random.fold_in(arg_keys[8], part), 9)
    feats = normal_values(part_splits[0], (VERTS, H), 1.0, 6.0, ((0, 8), (1, 2)))
    tiles = normal_values(part_splits[1], (RBLK, K, 128, 128), (128 * K) ** -0.5, 0.125, ((0, 8),))
    tile_cols = draw_tile_cols(jax.random.fold_in(jax.random.fold_in(arg_keys[8], part), 71), part)
    sends = draw_sends(jax.random.fold_in(jax.random.fold_in(arg_keys[8], part), 71), part)
    pins = draw_pins(jax.random.fold_in(jax.random.fold_in(arg_keys[8], part), 71), part)
    weight = normal_values(arg_keys[5], (H, H), H ** -0.5, 0.25, ((1, 2),))
    bias = normal_values(arg_keys[6], (H,), 0.5, 3.0, ((0, 2),), jnp.float32)
    cotan = normal_values(part_splits[7], (VERTS, H), 1.0, 6.0, ((0, 8), (1, 2)))
    return {"feats": feats, "tiles": tiles, "tile_cols": tile_cols, "sends": sends, "pins": pins, "weight": weight, "bias": bias, "cotan": cotan}


def partners(shift):
    return jnp.bitwise_xor(jnp.arange(N_DOM, dtype=jnp.int32), jnp.int32(1 << shift))

def reference(feats, tiles, tile_cols, sends, pins, weight, bias, cotan):
    nbits = N_DOM.bit_length() - 1
    shifts = (0, nbits // 2, nbits - 1)
    blocks = feats.reshape(N_DOM, BLOCKS_DEV, 128, H)
    tile_dev = tiles.reshape(N_DOM, BLOCKS_DEV, K, 128, 128)
    cols_dev = tile_cols.reshape(N_DOM, BLOCKS_DEV, K)
    received = []
    for m in range(3):
        mate = partners(shifts[m])
        chosen = jax.vmap(lambda one, idx: one[idx])(blocks, sends[:, m, :])
        received.append(chosen[mate])
    sources = jnp.concatenate([blocks] + received, axis=1)

    def aggregate(items):
        tile_one, cols_one, src_one = items
        picked = src_one[cols_one]
        return jnp.einsum('rkij,rkjh->rih', tile_one.astype(jnp.float32), picked.astype(jnp.float32))
    agg = lax.map(aggregate, (tile_dev, cols_dev, sources)).astype(jnp.bfloat16).reshape(VERTS, H)
    pre = jnp.dot(agg, weight, preferred_element_type=jnp.float32) + bias
    local_ids = jnp.arange(VERT_DEV, dtype=jnp.int32)
    pinned = jnp.any(local_ids[None, :, None] == pins[:, None, :], axis=2).reshape(VERTS)
    keep = 1.0 - pinned.astype(jnp.float32)
    sig = jax.nn.sigmoid(pre)
    out = (feats.astype(jnp.float32) + keep[:, None] * pre * sig).astype(jnp.bfloat16)
    dpre = (keep[:, None] * cotan.astype(jnp.float32) * sig * (1.0 + pre * (1.0 - sig))).astype(jnp.bfloat16)
    scale = 1.0 / math.sqrt(VERTS)
    dweight = jnp.dot(agg.T, dpre, preferred_element_type=jnp.float32) * scale
    dbias = lax.optimization_barrier(jnp.sum(dpre.astype(jnp.float32), axis=0)) * scale
    dagg = jnp.dot(dpre, weight.T, preferred_element_type=jnp.float32).astype(jnp.bfloat16)
    dblocks = dagg.reshape(N_DOM, BLOCKS_DEV, 128, H)

    def spread(items):
        tile_one, cols_one, grad_one = items
        prod = jnp.einsum('rkij,rih->rkjh', tile_one.astype(jnp.float32), grad_one.astype(jnp.float32))
        onehot = (cols_one.reshape(-1)[:, None] == jnp.arange(SOURCES, dtype=jnp.int32)[None, :]).astype(jnp.float32)
        return jnp.einsum('ns,njh->sjh', onehot, prod.reshape(BLOCKS_DEV * K, 128, H), precision=lax.Precision.HIGHEST)
    dsrc = lax.map(spread, (tile_dev, cols_dev, dblocks))
    own = dsrc[:, :BLOCKS_DEV]
    for m in range(3):
        mate = partners(shifts[m])
        back = dsrc[:, BLOCKS_DEV + m * SEND_BLOCKS:BLOCKS_DEV + (m + 1) * SEND_BLOCKS][mate]
        onehot = (sends[:, m, :, None] == jnp.arange(BLOCKS_DEV, dtype=jnp.int32)[None, None, :]).astype(jnp.float32)
        own = own + jnp.einsum('ejr,ejih->erih', onehot, back, precision=lax.Precision.HIGHEST)
    dfeat = (cotan.astype(jnp.float32) + own.reshape(VERTS, H)).astype(jnp.bfloat16)
    return (out, dfeat, dweight, dbias)
```

```python
import functools
import math

import jax
import jax.numpy as jnp
from jax import lax
from jax.experimental import pallas as pl
from jax.experimental.pallas import tpu as pltpu
from jax.sharding import PartitionSpec as P

BLK = 128
VMEM = pltpu.VMEM


def swapped(block, axis, distance):
    count = lax.axis_size(axis)
    route = []
    for low in range(count):
        high = low | 1 << distance
        if high != low and high < count:
            route += [(low, high), (high, low)]
    return lax.ppermute(block, axis, route)


def whole(shape):
    return pl.BlockSpec(shape, lambda *_: (0,) * len(shape))


def params(mib, count=1):
    return pltpu.CompilerParams(
        vmem_limit_bytes=mib << 20, dimension_semantics=("arbitrary",) * count
    )


def pick_kernel(nsend, sends_ref, feats_ref, *out_refs):
    for m in range(3):
        for j in range(nsend):
            out_refs[m][j] = feats_ref[sends_ref[m * nsend + j]]


def pick_call(blocks, sends):
    nblock, _, width = blocks.shape
    nsend = sends.shape[2]
    return pl.pallas_call(
        functools.partial(pick_kernel, nsend),
        grid_spec=pltpu.PrefetchScalarGridSpec(
            num_scalar_prefetch=1,
            grid=(1,),
            in_specs=[whole((nblock, BLK, width))],
            out_specs=[whole((nsend, BLK, width))] * 3,
        ),
        out_shape=[jax.ShapeDtypeStruct((nsend, BLK, width), blocks.dtype)] * 3,
        compiler_params=params(16),
        name="pick",
    )(sends.reshape(-1), blocks)


def agg_kernel(ntile, nblock, nsend, cols_ref, tiles_ref, own_ref, r0, r1, r2, agg_ref, src, sems):
    r = pl.program_id(0)

    @pl.when(r == 0)
    def _():
        copies = [pltpu.make_async_copy(own_ref, src.at[pl.ds(0, nblock)], sems.at[0])]
        for m, ref in enumerate((r0, r1, r2)):
            copies.append(
                pltpu.make_async_copy(
                    ref, src.at[pl.ds(nblock + m * nsend, nsend)], sems.at[m + 1]
                )
            )
        for copy in copies:
            copy.start()
        for copy in copies:
            copy.wait()

    lhs = jnp.concatenate([tiles_ref[0, k] for k in range(ntile)], axis=1)
    rhs = jnp.concatenate([src[cols_ref[r * ntile + k]] for k in range(ntile)], axis=0)
    agg_ref[...] = jnp.dot(lhs, rhs, preferred_element_type=jnp.float32).astype(agg_ref.dtype)


def agg_call(tiles, cols, blocks, received):
    nblock, ntile = tiles.shape[:2]
    width = blocks.shape[2]
    nsend = received[0].shape[0]
    anywhere = pl.BlockSpec(memory_space=pl.ANY)
    return pl.pallas_call(
        functools.partial(agg_kernel, ntile, nblock, nsend),
        grid_spec=pltpu.PrefetchScalarGridSpec(
            num_scalar_prefetch=1,
            grid=(nblock,),
            in_specs=[pl.BlockSpec((1, ntile, BLK, BLK), lambda r, _: (r, 0, 0, 0))]
            + [anywhere] * 4,
            out_specs=pl.BlockSpec((BLK, width), lambda r, _: (r, 0)),
            scratch_shapes=[
                VMEM((nblock + 3 * nsend, BLK, width), blocks.dtype),
                pltpu.SemaphoreType.DMA((4,)),
            ],
        ),
        out_shape=jax.ShapeDtypeStruct((nblock * BLK, width), blocks.dtype),
        compiler_params=params(24),
        name="agg",
    )(cols, tiles, blocks, *received)


TRANS = (((1,), (1,)), ((), ()))
DEEP = (((0,), (0,)), ((), ()))


def mid_kernel(mine_ref, other_ref, w_ref, bias_ref, pins_ref, feats_ref, cotan_ref, out_ref, dpre_ref, wb_ref):
    step = pl.program_id(0)
    chunk, width = feats_ref.shape
    hid = lax.axis_index("hid")
    here = pl.ds(pl.multiple_of(hid * width, width), width)
    there = pl.ds(pl.multiple_of((1 - hid) * width, width), width)
    mine, other = mine_ref[...], other_ref[...]
    pre = (
        jnp.dot(mine, w_ref[here, :], preferred_element_type=jnp.float32)
        + jnp.dot(other, w_ref[there, :], preferred_element_type=jnp.float32)
        + bias_ref[...]
    )
    ids = lax.broadcasted_iota(jnp.int32, (chunk, pins_ref.shape[1]), 0) + step * chunk
    hit = jnp.where(ids == pins_ref[...], 1.0, 0.0)
    keep = 1.0 - jnp.max(hit, axis=1, keepdims=True)
    sig = jax.nn.sigmoid(pre)
    out_ref[...] = (feats_ref[...].astype(jnp.float32) + keep * pre * sig).astype(out_ref.dtype)
    dpre = (
        keep * cotan_ref[...].astype(jnp.float32) * sig * (1.0 + pre * (1.0 - sig))
    ).astype(dpre_ref.dtype)
    dpre_ref[...] = dpre

    @pl.when(step == 0)
    def _():
        wb_ref[...] = jnp.zeros_like(wb_ref)

    wb_ref[here, :] += lax.dot_general(mine, dpre, DEEP, preferred_element_type=jnp.float32)
    wb_ref[there, :] += lax.dot_general(other, dpre, DEEP, preferred_element_type=jnp.float32)
    folded = jnp.sum(dpre.astype(jnp.float32).reshape(chunk // 8, 8, width), axis=0)
    wb_ref[2 * width :, :] += folded


def mid_call(mine, other, weight, bias, pins, feats, cotan):
    rows, width = feats.shape
    chunk = 256
    rowed = pl.BlockSpec((chunk, width), lambda i: (i, 0))
    return pl.pallas_call(
        mid_kernel,
        grid=(rows // chunk,),
        in_specs=[
            rowed,
            rowed,
            whole(weight.shape),
            whole((1, width)),
            whole(pins.shape),
            rowed,
            rowed,
        ],
        out_specs=[rowed, rowed, whole((2 * width + 8, width))],
        out_shape=[
            jax.ShapeDtypeStruct((rows, width), feats.dtype),
            jax.ShapeDtypeStruct((rows, width), feats.dtype),
            jax.ShapeDtypeStruct((2 * width + 8, width), jnp.float32),
        ],
        compiler_params=params(24),
        name="mid",
    )(mine, other, weight, bias.reshape(1, width), pins, feats, cotan)


def spread_kernel(ntile, nblock, cols_ref, tiles_ref, mine_ref, other_ref, w_ref, wx_ref, own_ref, b0, b1, b2, acc):
    r = pl.program_id(0)
    width = mine_ref.shape[1]
    nsend = b0.shape[0]

    @pl.when(r == 0)
    def _():
        acc[...] = jnp.zeros_like(acc)

    hid = lax.axis_index("hid")
    here = pl.ds(pl.multiple_of(hid * width, width), width)
    dagg = (
        lax.dot_general(mine_ref[...], w_ref[here, :], TRANS, preferred_element_type=jnp.float32)
        + lax.dot_general(other_ref[...], wx_ref[...], TRANS, preferred_element_type=jnp.float32)
    ).astype(mine_ref.dtype)
    for k in range(ntile):
        acc[cols_ref[r * ntile + k]] += lax.dot_general(
            tiles_ref[0, k], dagg, DEEP, preferred_element_type=jnp.float32
        )

    @pl.when(r == nblock - 1)
    def _():
        own_ref[...] = acc[0:nblock]
        for m, ref in enumerate((b0, b1, b2)):
            ref[...] = acc[nblock + m * nsend : nblock + (m + 1) * nsend].astype(ref.dtype)


def spread_call(tiles, cols, mine, other, weight, wx, nsend):
    nblock, ntile = tiles.shape[:2]
    width = mine.shape[1]
    rowed = pl.BlockSpec((BLK, width), lambda r, _: (r, 0))
    return pl.pallas_call(
        functools.partial(spread_kernel, ntile, nblock),
        grid_spec=pltpu.PrefetchScalarGridSpec(
            num_scalar_prefetch=1,
            grid=(nblock,),
            in_specs=[
                pl.BlockSpec((1, ntile, BLK, BLK), lambda r, _: (r, 0, 0, 0)),
                rowed,
                rowed,
                whole(weight.shape),
                whole(wx.shape),
            ],
            out_specs=[whole((nblock, BLK, width))] + [whole((nsend, BLK, width))] * 3,
            scratch_shapes=[VMEM((nblock + 3 * nsend, BLK, width), jnp.float32)],
        ),
        out_shape=[jax.ShapeDtypeStruct((nblock, BLK, width), jnp.float32)]
        + [jax.ShapeDtypeStruct((nsend, BLK, width), mine.dtype)] * 3,
        compiler_params=params(32),
        name="spread",
    )(cols, tiles, mine, other, weight, wx)


def final_kernel(sends_ref, own_ref, cotan_ref, b0, b1, b2, out_ref, acc):
    nsend = b0.shape[0]
    acc[...] = own_ref[...] + cotan_ref[...].astype(jnp.float32)
    for m, ref in enumerate((b0, b1, b2)):
        for j in range(nsend):
            acc[sends_ref[m * nsend + j]] += ref[j].astype(jnp.float32)
    out_ref[...] = acc[...].astype(out_ref.dtype)


def final_call(sends, own, cotan, backs):
    shape = own.shape
    return pl.pallas_call(
        final_kernel,
        grid_spec=pltpu.PrefetchScalarGridSpec(
            num_scalar_prefetch=1,
            grid=(1,),
            in_specs=[whole(shape)] * 2 + [whole(backs[0].shape)] * 3,
            out_specs=whole(shape),
            scratch_shapes=[VMEM(shape, jnp.float32)],
        ),
        out_shape=jax.ShapeDtypeStruct(shape, cotan.dtype),
        compiler_params=params(24),
        name="final",
    )(sends.reshape(-1), own, cotan.reshape(shape), *backs)


def body(feats, tiles, tile_cols, sends, pins, weight, bias, cotan):
    rows, width = feats.shape
    nblock = rows // BLK
    nsend = sends.shape[2]
    parts = lax.axis_size("dom")
    nbits = parts.bit_length() - 1
    shifts = (0, nbits // 2, nbits - 1)
    hid = lax.axis_index("hid")
    cols = tile_cols.reshape(-1)
    blocks = feats.reshape(nblock, BLK, width)
    picked = pick_call(blocks, sends)
    received = [swapped(picked[m], "dom", shifts[m]) for m in range(3)]
    wx = swapped(lax.dynamic_slice_in_dim(weight, (1 - hid) * width, width, 0), "hid", 0)
    agg = agg_call(tiles, cols, blocks, received)
    agg_other = swapped(agg, "hid", 0)
    out, dpre, wb = mid_call(agg, agg_other, weight, bias, pins, feats, cotan)
    dpre_other = swapped(dpre, "hid", 0)
    summed = lax.psum(wb, "dom")
    own, *outgoing = spread_call(tiles, cols, dpre, dpre_other, weight, wx, nsend)
    backs = [swapped(outgoing[m], "dom", shifts[m]) for m in range(3)]
    dfeat = final_call(sends, own, cotan, backs).reshape(rows, width)
    scale = 1.0 / math.sqrt(parts * rows)
    dweight = summed[: 2 * width] * scale
    dbias = jnp.sum(summed[2 * width :], axis=0) * scale
    return (out, dfeat, dweight, dbias)


def solution(mesh):
    return jax.shard_map(
        body,
        mesh=mesh,
        in_specs=(
            P(("basin", "dom"), "hid"),
            P(("basin", "dom"), None, None, None),
            P(("basin", "dom"), None),
            P(("basin", "dom"), None, None),
            P(("basin", "dom"), None),
            P(None, "hid"),
            P("hid"),
            P(("basin", "dom"), "hid"),
        ),
        out_specs=(
            P(("basin", "dom"), "hid"),
            P(("basin", "dom"), "hid"),
            P("basin", "hid"),
            P(("basin", "hid")),
        ),
        check_vma=False,
    )
```

```python
import functools
import math

import jax
import jax.numpy as jnp
from jax import lax
from jax.experimental import pallas as pl
from jax.experimental.pallas import tpu as pltpu
from jax.sharding import PartitionSpec as P

BLK = 128
VMEM = pltpu.VMEM


def swapped(block, axis, distance):
    count = lax.axis_size(axis)
    route = []
    for low in range(count):
        high = low | 1 << distance
        if high != low and high < count:
            route += [(low, high), (high, low)]
    return lax.ppermute(block, axis, route)


def whole(shape):
    return pl.BlockSpec(shape, lambda *_: (0,) * len(shape))


def params(mib, count=1):
    return pltpu.CompilerParams(
        vmem_limit_bytes=mib << 20, dimension_semantics=("arbitrary",) * count
    )


MESH = pl.DeviceIdType.MESH
SMEM_SPEC = pl.BlockSpec(memory_space=pltpu.SMEM)
VMEM_SPEC = pl.BlockSpec(memory_space=pltpu.VMEM)
ANY_SPEC = pl.BlockSpec(memory_space=pl.ANY)


def greet(partners):
    barrier = pltpu.get_barrier_semaphore()
    for axis, mate in partners:
        pl.semaphore_signal(barrier, inc=1, device_id={axis: mate}, device_id_type=MESH)
    pl.semaphore_wait(barrier, len(partners))


def flipped(index, bit):
    return index + (1 - 2 * ((index // (1 << bit)) % 2)) * (1 << bit)


def front_kernel(shifts, cols_ref, sends_ref, feats_ref, tiles_ref, agg_ref, held, src, outbox, tile_sem, send_sems, recv_sems):
    nblock, ntile = held.shape[:2]
    nsend = outbox.shape[1]
    me = lax.axis_index("dom")
    fetch = pltpu.make_async_copy(tiles_ref, held, tile_sem)
    fetch.start()
    mates = [flipped(me, shift) for shift in shifts]
    greet([("dom", mate) for mate in mates])
    copies = []
    for m in (2, 1, 0):
        for j in range(nsend):
            outbox[m, j] = feats_ref[sends_ref[m * nsend + j]]
        copy = pltpu.make_async_remote_copy(
            src_ref=outbox.at[m],
            dst_ref=src.at[pl.ds(nblock + m * nsend, nsend)],
            send_sem=send_sems.at[m],
            recv_sem=recv_sems.at[m],
            device_id={"dom": mates[m]},
            device_id_type=MESH,
        )
        copy.start()
        copies.append(copy)
    src[0:nblock] = feats_ref[...]
    fetch.wait()
    for copy in copies:
        copy.wait()

    def one_row(r, carry):
        lhs = jnp.concatenate([held[r, k] for k in range(ntile)], axis=1)
        rhs = jnp.concatenate([src[cols_ref[r * ntile + k]] for k in range(ntile)], axis=0)
        agg_ref[r] = jnp.dot(lhs, rhs, preferred_element_type=jnp.float32).astype(agg_ref.dtype)
        return carry

    lax.fori_loop(0, nblock, one_row, 0)


def front_call(tiles, cols, sends, blocks, shifts):
    nblock, _, width = blocks.shape
    nsend = sends.shape[2]
    return pl.pallas_call(
        functools.partial(front_kernel, shifts),
        in_specs=[SMEM_SPEC, SMEM_SPEC, VMEM_SPEC, ANY_SPEC],
        out_specs=VMEM_SPEC,
        out_shape=jax.ShapeDtypeStruct(blocks.shape, blocks.dtype),
        scratch_shapes=[
            VMEM(tiles.shape, tiles.dtype),
            VMEM((nblock + 3 * nsend, BLK, width), blocks.dtype),
            VMEM((3, nsend, BLK, width), blocks.dtype),
            pltpu.SemaphoreType.DMA,
            pltpu.SemaphoreType.DMA((3,)),
            pltpu.SemaphoreType.DMA((3,)),
        ],
        compiler_params=pltpu.CompilerParams(
            vmem_limit_bytes=56 << 20, collective_id=0, has_side_effects=True
        ),
        name="front",
    )(cols, sends.reshape(-1), blocks, tiles)


TRANS = (((1,), (1,)), ((), ()))
DEEP = (((0,), (0,)), ((), ()))


def mid_kernel(mine_ref, other_ref, w_ref, bias_ref, pins_ref, feats_ref, cotan_ref, out_ref, dpre_ref, wb_ref):
    step = pl.program_id(0)
    chunk, width = feats_ref.shape
    hid = lax.axis_index("hid")
    here = pl.ds(pl.multiple_of(hid * width, width), width)
    there = pl.ds(pl.multiple_of((1 - hid) * width, width), width)
    mine, other = mine_ref[...], other_ref[...]
    pre = (
        jnp.dot(mine, w_ref[here, :], preferred_element_type=jnp.float32)
        + jnp.dot(other, w_ref[there, :], preferred_element_type=jnp.float32)
        + bias_ref[...]
    )
    ids = lax.broadcasted_iota(jnp.int32, (chunk, pins_ref.shape[1]), 0) + step * chunk
    hit = jnp.where(ids == pins_ref[...], 1.0, 0.0)
    keep = 1.0 - jnp.max(hit, axis=1, keepdims=True)
    sig = jax.nn.sigmoid(pre)
    out_ref[...] = (feats_ref[...].astype(jnp.float32) + keep * pre * sig).astype(out_ref.dtype)
    dpre = (
        keep * cotan_ref[...].astype(jnp.float32) * sig * (1.0 + pre * (1.0 - sig))
    ).astype(dpre_ref.dtype)
    dpre_ref[...] = dpre

    @pl.when(step == 0)
    def _():
        wb_ref[...] = jnp.zeros_like(wb_ref)

    wb_ref[here, :] += lax.dot_general(mine, dpre, DEEP, preferred_element_type=jnp.float32)
    wb_ref[there, :] += lax.dot_general(other, dpre, DEEP, preferred_element_type=jnp.float32)
    folded = jnp.sum(dpre.astype(jnp.float32).reshape(chunk // 8, 8, width), axis=0)
    wb_ref[2 * width :, :] += folded


def mid_call(mine, other, weight, bias, pins, feats, cotan):
    rows, width = feats.shape
    chunk = 256
    rowed = pl.BlockSpec((chunk, width), lambda i: (i, 0))
    return pl.pallas_call(
        mid_kernel,
        grid=(rows // chunk,),
        in_specs=[
            rowed,
            rowed,
            whole(weight.shape),
            whole((1, width)),
            whole(pins.shape),
            rowed,
            rowed,
        ],
        out_specs=[rowed, rowed, whole((2 * width + 8, width))],
        out_shape=[
            jax.ShapeDtypeStruct((rows, width), feats.dtype),
            jax.ShapeDtypeStruct((rows, width), feats.dtype),
            jax.ShapeDtypeStruct((2 * width + 8, width), jnp.float32),
        ],
        compiler_params=params(56),
        name="mid",
    )(mine, other, weight, bias.reshape(1, width), pins, feats, cotan)


def spread_kernel(ntile, nblock, cols_ref, tiles_ref, mine_ref, other_ref, w_ref, wx_ref, own_ref, b0, b1, b2, acc):
    r = pl.program_id(0)
    width = mine_ref.shape[1]
    nsend = b0.shape[0]

    @pl.when(r == 0)
    def _():
        acc[...] = jnp.zeros_like(acc)

    hid = lax.axis_index("hid")
    here = pl.ds(pl.multiple_of(hid * width, width), width)
    dagg = (
        lax.dot_general(mine_ref[...], w_ref[here, :], TRANS, preferred_element_type=jnp.float32)
        + lax.dot_general(other_ref[...], wx_ref[...], TRANS, preferred_element_type=jnp.float32)
    ).astype(mine_ref.dtype)
    for k in range(ntile):
        acc[cols_ref[r * ntile + k]] += lax.dot_general(
            tiles_ref[0, k], dagg, DEEP, preferred_element_type=jnp.float32
        )

    @pl.when(r == nblock - 1)
    def _():
        own_ref[...] = acc[0:nblock]
        for m, ref in enumerate((b0, b1, b2)):
            ref[...] = acc[nblock + m * nsend : nblock + (m + 1) * nsend].astype(ref.dtype)


def spread_call(tiles, cols, mine, other, weight, wx, nsend):
    nblock, ntile = tiles.shape[:2]
    width = mine.shape[1]
    rowed = pl.BlockSpec((BLK, width), lambda r, _: (r, 0))
    return pl.pallas_call(
        functools.partial(spread_kernel, ntile, nblock),
        grid_spec=pltpu.PrefetchScalarGridSpec(
            num_scalar_prefetch=1,
            grid=(nblock,),
            in_specs=[
                pl.BlockSpec((1, ntile, BLK, BLK), lambda r, _: (r, 0, 0, 0)),
                rowed,
                rowed,
                whole(weight.shape),
                whole(wx.shape),
            ],
            out_specs=[whole((nblock, BLK, width))] + [whole((nsend, BLK, width))] * 3,
            scratch_shapes=[VMEM((nblock + 3 * nsend, BLK, width), jnp.float32)],
        ),
        out_shape=[jax.ShapeDtypeStruct((nblock, BLK, width), jnp.float32)]
        + [jax.ShapeDtypeStruct((nsend, BLK, width), mine.dtype)] * 3,
        compiler_params=params(56),
        name="spread",
    )(cols, tiles, mine, other, weight, wx)


def final_kernel(shifts, nbits, scale, inv_ref, own_ref, cotan_ref, b0, b1, b2, wb_ref, dfeat_ref, dw_ref, db_ref, acc, in0, in1, in2, wsum, outw, inw, gath, bsum, bin_, bsend, brecv, rsend, rrecv, gsend, grecv, vsend, vrecv):
    nblock = own_ref.shape[0]
    nsend = b0.shape[0]
    high = gath.shape[0]
    me = lax.axis_index("dom")
    greet([("dom", flipped(me, bit)) for bit in range(nbits)])

    def push(src, dst, send, recv, bit):
        copy = pltpu.make_async_remote_copy(
            src_ref=src,
            dst_ref=dst,
            send_sem=send,
            recv_sem=recv,
            device_id={"dom": flipped(me, bit)},
            device_id_type=MESH,
        )
        copy.start()
        return copy

    def wide(start, size):
        return pl.ds(pl.multiple_of(start, 16), size)

    boxes = (b0, b1, b2)
    inboxes = (in0, in1, in2)
    wsum[...] = wb_ref[0:high]
    bsum[...] = wb_ref[high : high + 8]
    start, size = me * 0, high
    at = 0
    backs = [None] * 3
    for bit in range(nbits):
        half = size // 2
        upper = (me // (1 << bit)) % 2
        give = start + (1 - upper) * half
        start = start + upper * half
        size = half
        outw[at : at + half] = wsum[wide(give, half)].astype(outw.dtype)
        copy = push(outw.at[pl.ds(at, half)], inw.at[pl.ds(at, half)], rsend.at[bit], rrecv.at[bit], bit)
        outgoing = bsum if bit == 0 else bin_.at[2 * bit - 1]
        bcopy = push(outgoing, bin_.at[2 * bit], vsend.at[bit], vrecv.at[bit], bit)
        if bit == 0:
            for m in (2, 1, 0):
                backs[m] = push(boxes[m], inboxes[m].at[pl.ds(0, nsend)], bsend.at[m], brecv.at[m], shifts[m])
            acc[...] = own_ref[...] + cotan_ref[...].astype(jnp.float32)
            for m in range(3):
                inboxes[m][nsend] = jnp.zeros(in0.shape[1:], in0.dtype)
        copy.wait()
        bcopy.wait()
        here = wide(start, half)
        wsum[here] += inw[at : at + half].astype(jnp.float32)
        bin_[2 * bit + 1] = outgoing[...] + bin_[2 * bit]
        at += half
    gath[wide(start, size)] = wsum[wide(start, size)].astype(gath.dtype)
    for bit in reversed(range(nbits)):
        here = wide(start, size)
        push(gath.at[here], gath.at[here], gsend.at[bit], grecv.at[bit], bit).wait()
        start = start - ((me // (1 << bit)) % 2) * size
        size = size * 2
    dw_ref[...] = gath[...].astype(jnp.float32) * scale
    db_ref[...] = jnp.sum(bin_[2 * nbits - 1], axis=0, keepdims=True) * scale
    for m in range(3):
        backs[m].wait()
        for b in range(nblock):
            total = acc[b] + inboxes[m][inv_ref[m * nblock + b]].astype(jnp.float32)
            if m < 2:
                acc[b] = total
            else:
                dfeat_ref[b] = total.astype(dfeat_ref.dtype)


def final_call(inv, own, cotan, outgoing, wb, shifts, nbits, scale):
    shape = own.shape
    nsend, _, width = outgoing[0].shape
    high = wb.shape[0] - 8
    sem = pltpu.SemaphoreType.DMA
    return pl.pallas_call(
        functools.partial(final_kernel, shifts, nbits, scale),
        in_specs=[SMEM_SPEC] + [VMEM_SPEC] * 6,
        out_specs=[VMEM_SPEC] * 3,
        out_shape=[
            jax.ShapeDtypeStruct(shape, cotan.dtype),
            jax.ShapeDtypeStruct((high, width), jnp.float32),
            jax.ShapeDtypeStruct((1, width), jnp.float32),
        ],
        scratch_shapes=[
            VMEM(shape, jnp.float32),
            VMEM((nsend + 1, BLK, width), cotan.dtype),
            VMEM((nsend + 1, BLK, width), cotan.dtype),
            VMEM((nsend + 1, BLK, width), cotan.dtype),
            VMEM((high, width), jnp.float32),
            VMEM((high, width), jnp.bfloat16),
            VMEM((high, width), jnp.bfloat16),
            VMEM((high, width), jnp.bfloat16),
            VMEM((8, width), jnp.float32),
            VMEM((2 * nbits, 8, width), jnp.float32),
            sem((3,)),
            sem((3,)),
            sem((nbits,)),
            sem((nbits,)),
            sem((nbits,)),
            sem((nbits,)),
            sem((nbits,)),
            sem((nbits,)),
        ],
        compiler_params=pltpu.CompilerParams(
            vmem_limit_bytes=56 << 20, collective_id=1, has_side_effects=True
        ),
        name="final",
    )(inv, own, cotan.reshape(shape), *outgoing, wb)


def body(feats, tiles, tile_cols, sends, pins, weight, bias, cotan):
    rows, width = feats.shape
    nblock = rows // BLK
    nsend = sends.shape[2]
    parts = lax.axis_size("dom")
    nbits = parts.bit_length() - 1
    shifts = (0, nbits // 2, nbits - 1)
    hid = lax.axis_index("hid")
    cols = tile_cols.reshape(-1)
    blocks = feats.reshape(nblock, BLK, width)
    hits = sends[0][:, :, None] == jnp.arange(nblock, dtype=jnp.int32)[None, None, :]
    ranks = jnp.arange(nsend, dtype=jnp.int32)[None, :, None] - nsend
    inv = (nsend + jnp.sum(jnp.where(hits, ranks, 0), axis=1)).reshape(-1)
    wx = swapped(lax.dynamic_slice_in_dim(weight, (1 - hid) * width, width, 0), "hid", 0)
    agg = front_call(tiles, cols, sends, blocks, shifts).reshape(rows, width)
    agg_other = swapped(agg, "hid", 0)
    out, dpre, wb = mid_call(agg, agg_other, weight, bias, pins, feats, cotan)
    dpre_other = swapped(dpre, "hid", 0)
    own, *outgoing = spread_call(tiles, cols, dpre, dpre_other, weight, wx, nsend)
    scale = 1.0 / math.sqrt(parts * rows)
    dfeat, dweight, dbias = final_call(inv, own, cotan, outgoing, wb, shifts, nbits, scale)
    return (out, dfeat.reshape(rows, width), dweight, dbias.reshape(-1))


def solution(mesh):
    return jax.shard_map(
        body,
        mesh=mesh,
        in_specs=(
            P(("basin", "dom"), "hid"),
            P(("basin", "dom"), None, None, None),
            P(("basin", "dom"), None),
            P(("basin", "dom"), None, None),
            P(("basin", "dom"), None),
            P(None, "hid"),
            P("hid"),
            P(("basin", "dom"), "hid"),
        ),
        out_specs=(
            P(("basin", "dom"), "hid"),
            P(("basin", "dom"), "hid"),
            P("basin", "hid"),
            P(("basin", "hid")),
        ),
        check_vma=False,
    )
```

```python
import functools
import math

import jax
import jax.numpy as jnp
from jax import lax
from jax.experimental import pallas as pl
from jax.experimental.pallas import tpu as pltpu
from jax.sharding import PartitionSpec as P

BLK = 128
VMEM = pltpu.VMEM


GROUP = 4
LANES = 512


MESH = pl.DeviceIdType.MESH
SMEM_SPEC = pl.BlockSpec(memory_space=pltpu.SMEM)
VMEM_SPEC = pl.BlockSpec(memory_space=pltpu.VMEM)
ANY_SPEC = pl.BlockSpec(memory_space=pl.ANY)


def greet(partners):
    barrier = pltpu.get_barrier_semaphore()
    for axis, mate in partners:
        pl.semaphore_signal(barrier, inc=1, device_id={axis: mate}, device_id_type=MESH)
    pl.semaphore_wait(barrier, len(partners))


def flipped(index, bit):
    return index + (1 - 2 * ((index // (1 << bit)) % 2)) * (1 << bit)


def slot_tables(crow, ccol, count, pad, ntile):
    total = ccol.shape[0]

    def iota(shape, dim):
        return lax.broadcasted_iota(jnp.int32, shape, dim)

    def picked(mask, values, axis):
        return jnp.sum(jnp.where(mask, values, 0.0), axis=axis, keepdims=True)

    def groups(n):
        return jnp.floor((n + (GROUP - 1.0)) * (1.0 / GROUP))

    lanes = iota((1, LANES), 1)
    q_row = groups(picked(iota((total, LANES), 1) == ccol, 1.0, 0))
    q_col = groups(picked(iota((count, total), 0) == crow, 1.0, 1))
    base_row = picked(iota((count, LANES), 0) < iota((count, LANES), 1), q_col, 0)
    base_col = picked(iota((count, LANES), 1) < iota((count, LANES), 0), q_row, 1)
    earlier = iota((total, total), 1) < iota((total, total), 0)
    rank = picked((ccol == crow) & earlier, 1.0, 1)
    base = picked(iota((total, LANES), 1) < ccol, q_row, 1)
    pos = (base * GROUP + rank).astype(jnp.int32)
    ids = iota((total, LANES), 0).astype(jnp.float32) - pad
    index = pad + picked(iota((total, LANES), 1) == pos, ids, 0)
    block = jnp.floor(index * (1.0 / ntile))
    last = base_row + q_row
    chain = 1.0 - picked(iota((count, LANES), 1) == base_col.astype(jnp.int32), 1.0, 0)
    rows = [index, block, last, chain] + [jnp.zeros((1, LANES), jnp.float32)] * 4
    return jnp.concatenate(rows, axis=0).astype(jnp.int32)


def front_kernel(shifts, cols_ref, crow_ref, ccol_ref, sends_ref, feats_ref, tiles_ref, agg_ref, other_ref, table_ref, held, src, outbox, tile_sem, send_sems, recv_sems, hsend, hrecv):
    nblock, ntile = held.shape[:2]
    nsend = outbox.shape[1]
    me = lax.axis_index("dom")
    fetch = pltpu.make_async_copy(tiles_ref, held, tile_sem)
    fetch.start()
    mates = [flipped(me, shift) for shift in shifts]
    peer = 1 - lax.axis_index("hid")
    greet([("dom", mate) for mate in mates] + [("hid", peer)])
    copies = []
    for m in (2, 1, 0):
        for j in range(nsend):
            outbox[m, j] = feats_ref[sends_ref[m * nsend + j]]
        copy = pltpu.make_async_remote_copy(
            src_ref=outbox.at[m],
            dst_ref=src.at[pl.ds(nblock + m * nsend, nsend)],
            send_sem=send_sems.at[m],
            recv_sem=recv_sems.at[m],
            device_id={"dom": mates[m]},
            device_id_type=MESH,
        )
        copy.start()
        copies.append(copy)
    src[0:nblock] = feats_ref[...]
    table_ref[...] = slot_tables(
        crow_ref[...], ccol_ref[...], src.shape[0], nblock * ntile, ntile
    )
    fetch.wait()
    for copy in copies:
        copy.wait()

    def one_row(r, carry):
        lhs = jnp.concatenate([held[r, k] for k in range(ntile)], axis=1)
        rhs = jnp.concatenate([src[cols_ref[r * ntile + k]] for k in range(ntile)], axis=0)
        agg_ref[r] = jnp.dot(lhs, rhs, preferred_element_type=jnp.float32).astype(agg_ref.dtype)
        return carry

    swaps = []
    count = hsend.shape[0]
    for c in range(count):
        lax.fori_loop(c * nblock // count, (c + 1) * nblock // count, one_row, 0)
        span = pl.ds(c * nblock // count, nblock // count)
        swap = pltpu.make_async_remote_copy(
            src_ref=agg_ref.at[span],
            dst_ref=other_ref.at[span],
            send_sem=hsend.at[c],
            recv_sem=hrecv.at[c],
            device_id={"hid": peer},
            device_id_type=MESH,
        )
        swap.start()
        swaps.append(swap)
    for swap in swaps:
        swap.wait()


def front_call(tiles, cols, sends, blocks, shifts):
    nblock, _, width = blocks.shape
    nsend = sends.shape[2]
    return pl.pallas_call(
        functools.partial(front_kernel, shifts),
        in_specs=[SMEM_SPEC, VMEM_SPEC, VMEM_SPEC, SMEM_SPEC, VMEM_SPEC, ANY_SPEC],
        out_specs=[VMEM_SPEC] * 3,
        out_shape=[
            jax.ShapeDtypeStruct(blocks.shape, blocks.dtype),
            jax.ShapeDtypeStruct(blocks.shape, blocks.dtype),
            jax.ShapeDtypeStruct((8, LANES), jnp.int32),
        ],
        scratch_shapes=[
            VMEM(tiles.shape, tiles.dtype),
            VMEM((nblock + 3 * nsend, BLK, width), blocks.dtype),
            VMEM((3, nsend, BLK, width), blocks.dtype),
            pltpu.SemaphoreType.DMA,
            pltpu.SemaphoreType.DMA((3,)),
            pltpu.SemaphoreType.DMA((3,)),
            pltpu.SemaphoreType.DMA((4,)),
            pltpu.SemaphoreType.DMA((4,)),
        ],
        compiler_params=pltpu.CompilerParams(
            vmem_limit_bytes=56 << 20, collective_id=0, has_side_effects=True
        ),
        name="front",
    )(cols, cols.reshape(1, -1), cols.reshape(-1, 1), sends.reshape(-1), blocks, tiles)


TRANS = (((1,), (1,)), ((), ()))
DEEP = (((0,), (0,)), ((), ()))


def rear_kernel(shifts, nbits, ntile, table, inv_ref, pins_ref, mine_ref, other_ref, w_ref, bias_ref, feats_ref, cotan_ref, tiles_ref, out_ref, dfeat_ref, dw_ref, db_ref, held, buf, dagg, dpre, dother, wx, b0, b1, b2, in0, in1, in2, wsum, outw, inw, gath, bsum, btmp, fetch_sem, xsend, xrecv, hsend, hrecv, bsend, brecv, rsend, rrecv, gsend, grecv, vsend, vrecv):
    nblock, _, width = dfeat_ref.shape
    rows = nblock * BLK
    ntiles = nblock * ntile
    slots = buf.shape[0] - 1
    nsend = b0.shape[0]
    high = gath.shape[0]
    me = lax.axis_index("dom")
    hid = lax.axis_index("hid")
    peer = 1 - hid
    fetch = pltpu.make_async_copy(tiles_ref, held.at[pl.ds(0, ntiles)], fetch_sem)
    fetch.start()
    greet([("dom", flipped(me, bit)) for bit in range(nbits)] + [("hid", peer)])

    def push(src, dst, send, recv, where):
        copy = pltpu.make_async_remote_copy(
            src_ref=src,
            dst_ref=dst,
            send_sem=send,
            recv_sem=recv,
            device_id=where,
            device_id_type=MESH,
        )
        copy.start()
        return copy

    def mate(bit):
        return {"dom": flipped(me, bit)}

    def wide(start, size):
        return pl.ds(pl.multiple_of(start, 16), size)

    here = wide(hid * width, width)
    there = wide(peer * width, width)
    wcopy = push(w_ref.at[there], wx, xsend, xrecv, {"hid": peer})
    wsum[...] = jnp.zeros_like(wsum)
    bsum[...] = jnp.zeros_like(bsum)
    chunk = 256

    def middle(i, carry):
        span = wide(i * chunk, chunk)
        mine, other = mine_ref[span, :], other_ref[span, :]
        pre = (
            jnp.dot(mine, w_ref[here, :], preferred_element_type=jnp.float32)
            + jnp.dot(other, w_ref[there, :], preferred_element_type=jnp.float32)
            + bias_ref[...]
        )
        ids = lax.broadcasted_iota(jnp.int32, (chunk, pins_ref.shape[1]), 0) + i * chunk
        hit = jnp.where(ids == pins_ref[...], 1.0, 0.0)
        keep = 1.0 - jnp.max(hit, axis=1, keepdims=True)
        sig = jax.nn.sigmoid(pre)
        out_ref[span, :] = (feats_ref[span, :].astype(jnp.float32) + keep * pre * sig).astype(
            out_ref.dtype
        )
        grad = (
            keep * cotan_ref[span, :].astype(jnp.float32) * sig * (1.0 + pre * (1.0 - sig))
        ).astype(dpre.dtype)
        dpre[span, :] = grad
        wsum[here, :] += lax.dot_general(mine, grad, DEEP, preferred_element_type=jnp.float32)
        wsum[there, :] += lax.dot_general(other, grad, DEEP, preferred_element_type=jnp.float32)
        bsum[...] += jnp.sum(grad.astype(jnp.float32).reshape(chunk // 8, 8, width), axis=0)
        return carry

    nchunk = hsend.shape[0]
    part = rows // nchunk
    swaps = []
    for c in range(nchunk):
        lax.fori_loop(c * part // chunk, (c + 1) * part // chunk, middle, 0)
        span = pl.ds(c * part, part)
        swaps.append(push(dpre.at[span], dother.at[span], hsend.at[c], hrecv.at[c], {"hid": peer}))

    state = {"start": me * 0, "size": high, "at": 0}

    def reduce_start(bit):
        half = state["size"] // 2
        upper = (me // (1 << bit)) % 2
        give = state["start"] + (1 - upper) * half
        state["start"] = state["start"] + upper * half
        state["size"] = half
        at = state["at"]
        outw[at : at + half] = wsum[wide(give, half)].astype(outw.dtype)
        outgoing = bsum if bit == 0 else btmp.at[2 * bit - 1]
        return (
            push(outw.at[pl.ds(at, half)], inw.at[pl.ds(at, half)], rsend.at[bit], rrecv.at[bit], mate(bit)),
            push(outgoing, btmp.at[2 * bit], vsend.at[bit], vrecv.at[bit], mate(bit)),
        )

    def reduce_end(bit, copies):
        for copy in copies:
            copy.wait()
        half, at = state["size"], state["at"]
        wsum[wide(state["start"], half)] += inw[at : at + half].astype(jnp.float32)
        outgoing = bsum[...] if bit == 0 else btmp[2 * bit - 1]
        btmp[2 * bit + 1] = outgoing + btmp[2 * bit]
        state["at"] = at + half
        if bit == nbits - 1:
            span = wide(state["start"], half)
            gath[span] = wsum[span].astype(gath.dtype)

    def gather_start(bit):
        span = wide(state["start"], state["size"])
        return (push(gath.at[span], gath.at[span], gsend.at[bit], grecv.at[bit], mate(bit)),)

    def gather_end(bit, copies):
        for copy in copies:
            copy.wait()
        state["start"] = state["start"] - ((me // (1 << bit)) % 2) * state["size"]
        state["size"] = state["size"] * 2

    stages = [(reduce_start, reduce_end, bit) for bit in range(nbits)]
    stages += [(gather_start, gather_end, bit) for bit in reversed(range(nbits))]

    flying = stages[0][0](stages[0][2])
    dagg[nblock] = jnp.zeros(dagg.shape[1:], dagg.dtype)
    held[ntiles] = jnp.zeros(held.shape[1:], held.dtype)
    buf[0] = jnp.zeros(buf.shape[1:], buf.dtype)
    for m, ref in enumerate((in0, in1, in2)):
        ref[nsend] = jnp.zeros(ref.shape[1:], ref.dtype)
    wcopy.wait()

    def undo(r, carry):
        span = wide(r * BLK, BLK)
        dagg[r] = (
            lax.dot_general(dpre[span, :], w_ref[here, :], TRANS, preferred_element_type=jnp.float32)
            + lax.dot_general(dother[span, :], wx[...], TRANS, preferred_element_type=jnp.float32)
        ).astype(dagg.dtype)
        return carry

    for c in range(nchunk):
        swaps[c].wait()
        lax.fori_loop(c * nblock // nchunk, (c + 1) * nblock // nchunk, undo, 0)
    fetch.wait()

    def one_slot(n, carry):
        lhs = jnp.concatenate([held[table[0, n * GROUP + g]] for g in range(GROUP)], axis=0)
        rhs = jnp.concatenate([dagg[table[1, n * GROUP + g]] for g in range(GROUP)], axis=0)
        prod = lax.dot_general(lhs, rhs, DEEP, preferred_element_type=jnp.float32)
        buf[n + 1] = buf[n] * table[3, n].astype(jnp.float32) + prod
        return carry

    nstage = len(stages)
    for i in range(nstage):
        lax.fori_loop(i * slots // nstage, (i + 1) * slots // nstage, one_slot, 0)
        stages[i][1](stages[i][2], flying)
        if i + 1 < nstage:
            flying = stages[i + 1][0](stages[i + 1][2])

    boxes = (b0, b1, b2)
    inboxes = (in0, in1, in2)
    backs = [None] * 3
    for m in (2, 1, 0):
        for j in range(nsend):
            boxes[m][j] = buf[table[2, nblock + m * nsend + j]].astype(b0.dtype)
        backs[m] = push(boxes[m], inboxes[m].at[pl.ds(0, nsend)], bsend.at[m], brecv.at[m], mate(shifts[m]))
    scale = 1.0 / math.sqrt((1 << nbits) * rows)
    dw_ref[...] = gath[...].astype(jnp.float32) * scale
    db_ref[...] = jnp.sum(btmp[2 * nbits - 1], axis=0, keepdims=True) * scale
    acc = []
    for m in range(3):
        backs[m].wait()
    for b in range(nblock):
        total = buf[table[2, b]] + cotan_ref[b * BLK : (b + 1) * BLK, :].astype(jnp.float32)
        for m in range(3):
            total = total + inboxes[m][inv_ref[m * nblock + b]].astype(jnp.float32)
        dfeat_ref[b] = total.astype(dfeat_ref.dtype)


def rear_call(table, inv, pins, mine, other, weight, bias, feats, cotan, tiles, nsend, shifts, nbits):
    rows, width = feats.shape
    nblock, ntile = tiles.shape[:2]
    ntiles = nblock * ntile
    high = weight.shape[0]
    slots = (ntiles + (GROUP - 1) * (nblock + 3 * nsend)) // GROUP
    sem = pltpu.SemaphoreType.DMA
    half = feats.dtype
    return pl.pallas_call(
        functools.partial(rear_kernel, shifts, nbits, ntile),
        in_specs=[SMEM_SPEC] * 2 + [VMEM_SPEC] * 7 + [ANY_SPEC],
        out_specs=[VMEM_SPEC] * 4,
        out_shape=[
            jax.ShapeDtypeStruct((rows, width), half),
            jax.ShapeDtypeStruct((nblock, BLK, width), half),
            jax.ShapeDtypeStruct((high, width), jnp.float32),
            jax.ShapeDtypeStruct((1, width), jnp.float32),
        ],
        scratch_shapes=[
            VMEM((ntiles + 1, BLK, BLK), half),
            VMEM((slots + 1, BLK, width), jnp.float32),
            VMEM((nblock + 1, BLK, width), half),
            VMEM((rows, width), half),
            VMEM((rows, width), half),
            VMEM((width, width), half),
        ]
        + [VMEM((nsend, BLK, width), half)] * 3
        + [VMEM((nsend + 1, BLK, width), half)] * 3
        + [VMEM((high, width), jnp.float32)]
        + [VMEM((high, width), half)] * 3
        + [
            VMEM((8, width), jnp.float32),
            VMEM((2 * nbits, 8, width), jnp.float32),
            sem,
            sem,
            sem,
            sem((4,)),
            sem((4,)),
            sem((3,)),
            sem((3,)),
        ]
        + [sem((nbits,))] * 6,
        compiler_params=pltpu.CompilerParams(
            vmem_limit_bytes=60 << 20, collective_id=1, has_side_effects=True
        ),
        name="rear",
    )(
        table,
        inv,
        pins,
        mine,
        other,
        weight,
        bias.reshape(1, width),
        feats,
        cotan,
        tiles.reshape(ntiles, BLK, BLK),
    )


def body(feats, tiles, tile_cols, sends, pins, weight, bias, cotan):
    rows, width = feats.shape
    nblock = rows // BLK
    nsend = sends.shape[2]
    nbits = lax.axis_size("dom").bit_length() - 1
    shifts = (0, nbits // 2, nbits - 1)
    blocks = feats.reshape(nblock, BLK, width)
    hits = sends[0][:, :, None] == jnp.arange(nblock, dtype=jnp.int32)[None, None, :]
    ranks = jnp.arange(nsend, dtype=jnp.int32)[None, :, None] - nsend
    inv = (nsend + jnp.sum(jnp.where(hits, ranks, 0), axis=1)).reshape(-1)
    agg, other, table = front_call(tiles, tile_cols.reshape(-1), sends, blocks, shifts)
    agg, other = agg.reshape(rows, width), other.reshape(rows, width)
    out, dfeat, dweight, dbias = rear_call(
        table, inv, pins, agg, other, weight, bias, feats, cotan, tiles, nsend, shifts, nbits
    )
    return (out, dfeat.reshape(rows, width), dweight, dbias.reshape(-1))


def solution(mesh):
    return jax.shard_map(
        body,
        mesh=mesh,
        in_specs=(
            P(("basin", "dom"), "hid"),
            P(("basin", "dom"), None, None, None),
            P(("basin", "dom"), None),
            P(("basin", "dom"), None, None),
            P(("basin", "dom"), None),
            P(None, "hid"),
            P("hid"),
            P(("basin", "dom"), "hid"),
        ),
        out_specs=(
            P(("basin", "dom"), "hid"),
            P(("basin", "dom"), "hid"),
            P("basin", "hid"),
            P(("basin", "hid")),
        ),
        check_vma=False,
    )
```

```python
import functools
import math

import jax
import jax.numpy as jnp
from jax import lax
from jax.experimental import pallas as pl
from jax.experimental.pallas import tpu as pltpu
from jax.sharding import PartitionSpec as P

BLK = 128
VMEM = pltpu.VMEM


GROUP = 4
LANES = 512


MESH = pl.DeviceIdType.MESH
SMEM_SPEC = pl.BlockSpec(memory_space=pltpu.SMEM)
VMEM_SPEC = pl.BlockSpec(memory_space=pltpu.VMEM)
ANY_SPEC = pl.BlockSpec(memory_space=pl.ANY)


def greet(partners):
    barrier = pltpu.get_barrier_semaphore()
    for axis, mate in partners:
        pl.semaphore_signal(barrier, inc=1, device_id={axis: mate}, device_id_type=MESH)
    pl.semaphore_wait(barrier, len(partners))


def flipped(index, bit):
    return index + (1 - 2 * ((index // (1 << bit)) % 2)) * (1 << bit)


def slot_tables(cols, sends_ref, count):
    nblock, ntile = cols.shape
    nsend = sends_ref.shape[2]
    total = nblock * ntile
    pad = total

    def iota(shape, dim):
        return lax.broadcasted_iota(jnp.int32, shape, dim)

    def picked(mask, values, axis):
        return jnp.sum(jnp.where(mask, values, 0.0), axis=axis, keepdims=True)

    def groups(n):
        return jnp.floor((n + (GROUP - 1.0)) * (1.0 / GROUP))

    flat = cols.astype(jnp.float32)
    deep = jnp.where(iota((total, nblock), 0) // ntile == iota((total, nblock), 1), 1.0, 0.0)
    wide = jnp.where(iota((ntile, total), 1) % ntile == iota((ntile, total), 0), 1.0, 0.0)
    tall = jnp.dot(deep, flat, preferred_element_type=jnp.float32)
    long = jnp.dot(flat, wide, preferred_element_type=jnp.float32)
    ccol = picked(iota((total, ntile), 0) % ntile == iota((total, ntile), 1), tall, 1)
    crow = picked(iota((nblock, total), 1) // ntile == iota((nblock, total), 0), long, 0)
    ccol, crow = ccol.astype(jnp.int32), crow.astype(jnp.int32)
    lanes = iota((1, LANES), 1)
    inverse = []
    for m in range(3):
        found = jnp.full((1, LANES), float(nsend), jnp.float32)
        for j in range(nsend):
            found = jnp.where(lanes == sends_ref[0, m, j], float(j), found)
        inverse.append(found)
    q_row = groups(picked(iota((total, LANES), 1) == ccol, 1.0, 0))
    q_col = groups(picked(iota((count, total), 0) == crow, 1.0, 1))
    base_row = picked(iota((count, LANES), 0) < iota((count, LANES), 1), q_col, 0)
    base_col = picked(iota((count, LANES), 1) < iota((count, LANES), 0), q_row, 1)
    earlier = iota((total, total), 1) < iota((total, total), 0)
    rank = picked((ccol == crow) & earlier, 1.0, 1)
    base = picked(iota((total, LANES), 1) < ccol, q_row, 1)
    pos = (base * GROUP + rank).astype(jnp.int32)
    ids = iota((total, LANES), 0).astype(jnp.float32) - pad
    index = pad + picked(iota((total, LANES), 1) == pos, ids, 0)
    block = jnp.floor(index * (1.0 / ntile))
    last = base_row + q_row
    chain = 1.0 - picked(iota((count, LANES), 1) == base_col.astype(jnp.int32), 1.0, 0)
    rows = [index, block, last, chain] + inverse + [jnp.zeros((1, LANES), jnp.float32)]
    return jnp.concatenate(rows, axis=0).astype(jnp.int32)


def front_kernel(shifts, cols_ref, cvec_ref, sends_ref, feats_ref, tiles_ref, agg_ref, other_ref, table_ref, held, src, outbox, tile_sem, send_sems, recv_sems, hsend, hrecv):
    nblock, ntile = held.shape[:2]
    nsend = outbox.shape[1]
    me = lax.axis_index("dom")
    fetch = pltpu.make_async_copy(tiles_ref, held, tile_sem)
    fetch.start()
    mates = [flipped(me, shift) for shift in shifts]
    peer = 1 - lax.axis_index("hid")
    greet([("dom", mate) for mate in mates] + [("hid", peer)])
    copies = []
    for m in (2, 1, 0):
        for j in range(nsend):
            outbox[m, j] = feats_ref[sends_ref[0, m, j]]
        copy = pltpu.make_async_remote_copy(
            src_ref=outbox.at[m],
            dst_ref=src.at[pl.ds(nblock + m * nsend, nsend)],
            send_sem=send_sems.at[m],
            recv_sem=recv_sems.at[m],
            device_id={"dom": mates[m]},
            device_id_type=MESH,
        )
        copy.start()
        copies.append(copy)
    src[0:nblock] = feats_ref[...]
    table_ref[...] = slot_tables(cvec_ref[...], sends_ref, src.shape[0])
    fetch.wait()
    for copy in copies:
        copy.wait()

    def one_row(r, carry):
        lhs = jnp.concatenate([held[r, k] for k in range(ntile)], axis=1)
        rhs = jnp.concatenate([src[cols_ref[r, k]] for k in range(ntile)], axis=0)
        agg_ref[r] = jnp.dot(lhs, rhs, preferred_element_type=jnp.float32).astype(agg_ref.dtype)
        return carry

    swaps = []
    count = hsend.shape[0]
    for c in range(count):
        lax.fori_loop(c * nblock // count, (c + 1) * nblock // count, one_row, 0)
        span = pl.ds(c * nblock // count, nblock // count)
        swap = pltpu.make_async_remote_copy(
            src_ref=agg_ref.at[span],
            dst_ref=other_ref.at[span],
            send_sem=hsend.at[c],
            recv_sem=hrecv.at[c],
            device_id={"hid": peer},
            device_id_type=MESH,
        )
        swap.start()
        swaps.append(swap)
    for swap in swaps:
        swap.wait()


def front_call(tiles, cols, sends, blocks, shifts):
    nblock, _, width = blocks.shape
    nsend = sends.shape[2]
    return pl.pallas_call(
        functools.partial(front_kernel, shifts),
        in_specs=[SMEM_SPEC, VMEM_SPEC, SMEM_SPEC, VMEM_SPEC, ANY_SPEC],
        out_specs=[VMEM_SPEC] * 3,
        out_shape=[
            jax.ShapeDtypeStruct(blocks.shape, blocks.dtype),
            jax.ShapeDtypeStruct(blocks.shape, blocks.dtype),
            jax.ShapeDtypeStruct((8, LANES), jnp.int32),
        ],
        scratch_shapes=[
            VMEM(tiles.shape, tiles.dtype),
            VMEM((nblock + 3 * nsend, BLK, width), blocks.dtype),
            VMEM((3, nsend, BLK, width), blocks.dtype),
            pltpu.SemaphoreType.DMA,
            pltpu.SemaphoreType.DMA((3,)),
            pltpu.SemaphoreType.DMA((3,)),
            pltpu.SemaphoreType.DMA((4,)),
            pltpu.SemaphoreType.DMA((4,)),
        ],
        compiler_params=pltpu.CompilerParams(
            vmem_limit_bytes=56 << 20, collective_id=0, has_side_effects=True
        ),
        name="front",
    )(cols, cols, sends, blocks, tiles)


TRANS = (((1,), (1,)), ((), ()))
DEEP = (((0,), (0,)), ((), ()))


def rear_kernel(shifts, nbits, ntile, table, pins_ref, mine_ref, other_ref, w_ref, bias_ref, feats_ref, cotan_ref, tiles_ref, out_ref, dfeat_ref, dw_ref, db_ref, held, buf, dagg, dpre, dother, wx, b0, b1, b2, in0, in1, in2, wsum, outw, inw, gath, bsum, btmp, fetch_sem, xsend, xrecv, hsend, hrecv, bsend, brecv, rsend, rrecv, gsend, grecv, vsend, vrecv):
    nblock, _, width = dfeat_ref.shape
    rows = nblock * BLK
    ntiles = nblock * ntile
    slots = buf.shape[0] - 1
    nsend = b0.shape[0]
    high = gath.shape[0]
    me = lax.axis_index("dom")
    hid = lax.axis_index("hid")
    peer = 1 - hid
    fetch = pltpu.make_async_copy(tiles_ref, held.at[pl.ds(0, ntiles)], fetch_sem)
    fetch.start()
    greet([("dom", flipped(me, bit)) for bit in range(nbits)] + [("hid", peer)])

    def push(src, dst, send, recv, where):
        copy = pltpu.make_async_remote_copy(
            src_ref=src,
            dst_ref=dst,
            send_sem=send,
            recv_sem=recv,
            device_id=where,
            device_id_type=MESH,
        )
        copy.start()
        return copy

    def mate(bit):
        return {"dom": flipped(me, bit)}

    def wide(start, size):
        return pl.ds(pl.multiple_of(start, 16), size)

    here = wide(hid * width, width)
    there = wide(peer * width, width)
    wcopy = push(w_ref.at[there], wx, xsend, xrecv, {"hid": peer})
    wsum[...] = jnp.zeros_like(wsum)
    bsum[...] = jnp.zeros_like(bsum)
    chunk = 256

    def middle(i, carry):
        span = wide(i * chunk, chunk)
        mine, other = mine_ref[span, :], other_ref[span, :]
        pre = (
            jnp.dot(mine, w_ref[here, :], preferred_element_type=jnp.float32)
            + jnp.dot(other, w_ref[there, :], preferred_element_type=jnp.float32)
            + bias_ref[...]
        )
        ids = lax.broadcasted_iota(jnp.int32, (chunk, pins_ref.shape[1]), 0) + i * chunk
        hit = jnp.where(ids == pins_ref[...], 1.0, 0.0)
        keep = 1.0 - jnp.max(hit, axis=1, keepdims=True)
        sig = jax.nn.sigmoid(pre)
        out_ref[span, :] = (feats_ref[span, :].astype(jnp.float32) + keep * pre * sig).astype(
            out_ref.dtype
        )
        grad = (
            keep * cotan_ref[span, :].astype(jnp.float32) * sig * (1.0 + pre * (1.0 - sig))
        ).astype(dpre.dtype)
        dpre[span, :] = grad
        wsum[here, :] += lax.dot_general(mine, grad, DEEP, preferred_element_type=jnp.float32)
        wsum[there, :] += lax.dot_general(other, grad, DEEP, preferred_element_type=jnp.float32)
        bsum[...] += jnp.sum(grad.astype(jnp.float32).reshape(chunk // 8, 8, width), axis=0)
        return carry

    nchunk = hsend.shape[0]
    part = rows // nchunk
    swaps = []
    for c in range(nchunk):
        lax.fori_loop(c * part // chunk, (c + 1) * part // chunk, middle, 0)
        span = pl.ds(c * part, part)
        swaps.append(push(dpre.at[span], dother.at[span], hsend.at[c], hrecv.at[c], {"hid": peer}))

    state = {"start": me * 0, "size": high, "at": 0}

    def reduce_start(bit):
        half = state["size"] // 2
        upper = (me // (1 << bit)) % 2
        give = state["start"] + (1 - upper) * half
        state["start"] = state["start"] + upper * half
        state["size"] = half
        at = state["at"]
        outw[at : at + half] = wsum[wide(give, half)].astype(outw.dtype)
        outgoing = bsum if bit == 0 else btmp.at[2 * bit - 1]
        return (
            push(outw.at[pl.ds(at, half)], inw.at[pl.ds(at, half)], rsend.at[bit], rrecv.at[bit], mate(bit)),
            push(outgoing, btmp.at[2 * bit], vsend.at[bit], vrecv.at[bit], mate(bit)),
        )

    def reduce_end(bit, copies):
        for copy in copies:
            copy.wait()
        half, at = state["size"], state["at"]
        wsum[wide(state["start"], half)] += inw[at : at + half].astype(jnp.float32)
        outgoing = bsum[...] if bit == 0 else btmp[2 * bit - 1]
        btmp[2 * bit + 1] = outgoing + btmp[2 * bit]
        state["at"] = at + half
        if bit == nbits - 1:
            span = wide(state["start"], half)
            gath[span] = wsum[span].astype(gath.dtype)

    def gather_start(bit):
        span = wide(state["start"], state["size"])
        return (push(gath.at[span], gath.at[span], gsend.at[bit], grecv.at[bit], mate(bit)),)

    def gather_end(bit, copies):
        for copy in copies:
            copy.wait()
        state["start"] = state["start"] - ((me // (1 << bit)) % 2) * state["size"]
        state["size"] = state["size"] * 2

    stages = [(reduce_start, reduce_end, bit) for bit in range(nbits)]
    stages += [(gather_start, gather_end, bit) for bit in reversed(range(nbits))]

    flying = stages[0][0](stages[0][2])
    dagg[nblock] = jnp.zeros(dagg.shape[1:], dagg.dtype)
    held[ntiles] = jnp.zeros(held.shape[1:], held.dtype)
    buf[0] = jnp.zeros(buf.shape[1:], buf.dtype)
    for m, ref in enumerate((in0, in1, in2)):
        ref[nsend] = jnp.zeros(ref.shape[1:], ref.dtype)
    wcopy.wait()

    def undo(r, carry):
        span = wide(r * BLK, BLK)
        dagg[r] = (
            lax.dot_general(dpre[span, :], w_ref[here, :], TRANS, preferred_element_type=jnp.float32)
            + lax.dot_general(dother[span, :], wx[...], TRANS, preferred_element_type=jnp.float32)
        ).astype(dagg.dtype)
        return carry

    done = 0
    for c in range(nchunk):
        swaps[c].wait()
        lax.fori_loop(c * nblock // nchunk, (c + 1) * nblock // nchunk, undo, 0)
        if c % 2 == 1 and done + 1 < len(stages):
            stages[done][1](stages[done][2], flying)
            done += 1
            flying = stages[done][0](stages[done][2])
    fetch.wait()

    def one_slot(n, carry):
        lhs = jnp.concatenate([held[table[0, n * GROUP + g]] for g in range(GROUP)], axis=0)
        rhs = jnp.concatenate([dagg[table[1, n * GROUP + g]] for g in range(GROUP)], axis=0)
        prod = lax.dot_general(lhs, rhs, DEEP, preferred_element_type=jnp.float32)
        buf[n + 1] = buf[n] * table[3, n].astype(jnp.float32) + prod
        return carry

    nstage = len(stages) - done
    for i in range(nstage):
        lax.fori_loop(i * slots // nstage, (i + 1) * slots // nstage, one_slot, 0)
        stages[done + i][1](stages[done + i][2], flying)
        if i + 1 < nstage:
            flying = stages[done + i + 1][0](stages[done + i + 1][2])

    boxes = (b0, b1, b2)
    inboxes = (in0, in1, in2)
    backs = [None] * 3
    for m in (2, 1, 0):
        for j in range(nsend):
            boxes[m][j] = buf[table[2, nblock + m * nsend + j]].astype(b0.dtype)
        backs[m] = push(boxes[m], inboxes[m].at[pl.ds(0, nsend)], bsend.at[m], brecv.at[m], mate(shifts[m]))
    scale = 1.0 / math.sqrt((1 << nbits) * rows)
    dw_ref[...] = gath[...].astype(jnp.float32) * scale
    db_ref[...] = jnp.sum(btmp[2 * nbits - 1], axis=0, keepdims=True) * scale
    acc = []
    for m in range(3):
        backs[m].wait()
    for b in range(nblock):
        total = buf[table[2, b]] + cotan_ref[b * BLK : (b + 1) * BLK, :].astype(jnp.float32)
        for m in range(3):
            total = total + inboxes[m][table[4 + m, b]].astype(jnp.float32)
        dfeat_ref[b] = total.astype(dfeat_ref.dtype)


def rear_call(table, pins, mine, other, weight, bias, feats, cotan, tiles, nsend, shifts, nbits):
    rows, width = feats.shape
    nblock, ntile = tiles.shape[:2]
    ntiles = nblock * ntile
    high = weight.shape[0]
    slots = (ntiles + (GROUP - 1) * (nblock + 3 * nsend)) // GROUP
    sem = pltpu.SemaphoreType.DMA
    half = feats.dtype
    return pl.pallas_call(
        functools.partial(rear_kernel, shifts, nbits, ntile),
        in_specs=[SMEM_SPEC] + [VMEM_SPEC] * 7 + [ANY_SPEC],
        out_specs=[VMEM_SPEC] * 4,
        out_shape=[
            jax.ShapeDtypeStruct((rows, width), half),
            jax.ShapeDtypeStruct((nblock, BLK, width), half),
            jax.ShapeDtypeStruct((high, width), jnp.float32),
            jax.ShapeDtypeStruct((1, width), jnp.float32),
        ],
        scratch_shapes=[
            VMEM((ntiles + 1, BLK, BLK), half),
            VMEM((slots + 1, BLK, width), jnp.float32),
            VMEM((nblock + 1, BLK, width), half),
            VMEM((rows, width), half),
            VMEM((rows, width), half),
            VMEM((width, width), half),
        ]
        + [VMEM((nsend, BLK, width), half)] * 3
        + [VMEM((nsend + 1, BLK, width), half)] * 3
        + [VMEM((high, width), jnp.float32)]
        + [VMEM((high, width), half)] * 3
        + [
            VMEM((8, width), jnp.float32),
            VMEM((2 * nbits, 8, width), jnp.float32),
            sem,
            sem,
            sem,
            sem((4,)),
            sem((4,)),
            sem((3,)),
            sem((3,)),
        ]
        + [sem((nbits,))] * 6,
        compiler_params=pltpu.CompilerParams(
            vmem_limit_bytes=60 << 20, collective_id=1, has_side_effects=True
        ),
        name="rear",
    )(
        table,
        pins,
        mine,
        other,
        weight,
        bias.reshape(1, width),
        feats,
        cotan,
        tiles.reshape(ntiles, BLK, BLK),
    )


def emit_kernel(*refs):
    count = len(refs) // 2
    sems = refs[-1]
    copies = [pltpu.make_async_copy(refs[i], refs[count + i], sems.at[i]) for i in range(count)]
    for copy in copies:
        copy.start()
    for copy in copies:
        copy.wait()


def emit_call(*arrays):
    count = len(arrays)
    return pl.pallas_call(
        emit_kernel,
        in_specs=[ANY_SPEC] * count,
        out_specs=[ANY_SPEC] * count,
        out_shape=[jax.ShapeDtypeStruct(one.shape, one.dtype) for one in arrays],
        scratch_shapes=[pltpu.SemaphoreType.DMA((count,))],
        name="emit",
    )(*arrays)


def body(feats, tiles, tile_cols, sends, pins, weight, bias, cotan):
    rows, width = feats.shape
    nblock = rows // BLK
    nsend = sends.shape[2]
    nbits = lax.axis_size("dom").bit_length() - 1
    shifts = (0, nbits // 2, nbits - 1)
    blocks = feats.reshape(nblock, BLK, width)
    agg, other, table = front_call(tiles, tile_cols, sends, blocks, shifts)
    agg, other = agg.reshape(rows, width), other.reshape(rows, width)
    out, dfeat, dweight, dbias = rear_call(
        table, pins, agg, other, weight, bias, feats, cotan, tiles, nsend, shifts, nbits
    )
    out, dfeat, dweight, dbias = emit_call(out, dfeat, dweight, dbias)
    return (out, dfeat.reshape(rows, width), dweight, dbias.reshape(-1))


def solution(mesh):
    return jax.shard_map(
        body,
        mesh=mesh,
        in_specs=(
            P(("basin", "dom"), "hid"),
            P(("basin", "dom"), None, None, None),
            P(("basin", "dom"), None),
            P(("basin", "dom"), None, None),
            P(("basin", "dom"), None),
            P(None, "hid"),
            P("hid"),
            P(("basin", "dom"), "hid"),
        ),
        out_specs=(
            P(("basin", "dom"), "hid"),
            P(("basin", "dom"), "hid"),
            P("basin", "hid"),
            P(("basin", "hid")),
        ),
        check_vma=False,
    )
```

```python
import functools
import math

import jax
import jax.numpy as jnp
from jax import lax
from jax.experimental import pallas as pl
from jax.experimental.pallas import tpu as pltpu
from jax.sharding import PartitionSpec as P

BLK = 128
VMEM = pltpu.VMEM


GROUP = 4
LANES = 512


MESH = pl.DeviceIdType.MESH
SMEM_SPEC = pl.BlockSpec(memory_space=pltpu.SMEM)
VMEM_SPEC = pl.BlockSpec(memory_space=pltpu.VMEM)
ANY_SPEC = pl.BlockSpec(memory_space=pl.ANY)


def greet(partners):
    barrier = pltpu.get_barrier_semaphore()
    for axis, mate in partners:
        pl.semaphore_signal(barrier, inc=1, device_id={axis: mate}, device_id_type=MESH)
    pl.semaphore_wait(barrier, len(partners))


def flipped(index, bit):
    return index + (1 - 2 * ((index // (1 << bit)) % 2)) * (1 << bit)


def slot_tables(cols, sends_ref, count):
    nblock, ntile = cols.shape
    nsend = sends_ref.shape[2]
    total = nblock * ntile
    pad = total

    def iota(shape, dim):
        return lax.broadcasted_iota(jnp.int32, shape, dim)

    def picked(mask, values, axis):
        return jnp.sum(jnp.where(mask, values, 0.0), axis=axis, keepdims=True)

    def groups(n):
        return jnp.floor((n + (GROUP - 1.0)) * (1.0 / GROUP))

    flat = cols.astype(jnp.float32)
    deep = jnp.where(iota((total, nblock), 0) // ntile == iota((total, nblock), 1), 1.0, 0.0)
    wide = jnp.where(iota((ntile, total), 1) % ntile == iota((ntile, total), 0), 1.0, 0.0)
    tall = jnp.dot(deep, flat, preferred_element_type=jnp.float32)
    long = jnp.dot(flat, wide, preferred_element_type=jnp.float32)
    ccol = picked(iota((total, ntile), 0) % ntile == iota((total, ntile), 1), tall, 1)
    crow = picked(iota((nblock, total), 1) // ntile == iota((nblock, total), 0), long, 0)
    ccol, crow = ccol.astype(jnp.int32), crow.astype(jnp.int32)
    lanes = iota((1, LANES), 1)
    inverse = []
    for m in range(3):
        found = jnp.full((1, LANES), float(nsend), jnp.float32)
        for j in range(nsend):
            found = jnp.where(lanes == sends_ref[0, m, j], float(j), found)
        inverse.append(found)
    q_row = groups(picked(iota((total, LANES), 1) == ccol, 1.0, 0))
    q_col = groups(picked(iota((count, total), 0) == crow, 1.0, 1))
    base_row = picked(iota((count, LANES), 0) < iota((count, LANES), 1), q_col, 0)
    base_col = picked(iota((count, LANES), 1) < iota((count, LANES), 0), q_row, 1)
    earlier = iota((total, total), 1) < iota((total, total), 0)
    rank = picked((ccol == crow) & earlier, 1.0, 1)
    base = picked(iota((total, LANES), 1) < ccol, q_row, 1)
    pos = (base * GROUP + rank).astype(jnp.int32)
    ids = iota((total, LANES), 0).astype(jnp.float32) - pad
    index = pad + picked(iota((total, LANES), 1) == pos, ids, 0)
    block = jnp.floor(index * (1.0 / ntile))
    last = base_row + q_row
    chain = 1.0 - picked(iota((count, LANES), 1) == base_col.astype(jnp.int32), 1.0, 0)
    rows = [index, block, last, chain] + inverse + [jnp.zeros((1, LANES), jnp.float32)]
    return jnp.concatenate(rows, axis=0).astype(jnp.int32)


def front_kernel(shifts, cols_ref, cvec_ref, sends_ref, feats_ref, tiles_ref, agg_ref, other_ref, table_ref, held, src, outbox, tile_sem, send_sems, recv_sems, hsend, hrecv):
    nblock, ntile = held.shape[:2]
    nsend = outbox.shape[1]
    me = lax.axis_index("dom")
    fetch = pltpu.make_async_copy(tiles_ref, held, tile_sem)
    fetch.start()
    mates = [flipped(me, shift) for shift in shifts]
    peer = 1 - lax.axis_index("hid")
    greet([("dom", mate) for mate in mates] + [("hid", peer)])
    copies = []
    for m in (2, 1, 0):
        for j in range(nsend):
            outbox[m, j] = feats_ref[sends_ref[0, m, j]]
        copy = pltpu.make_async_remote_copy(
            src_ref=outbox.at[m],
            dst_ref=src.at[pl.ds(nblock + m * nsend, nsend)],
            send_sem=send_sems.at[m],
            recv_sem=recv_sems.at[m],
            device_id={"dom": mates[m]},
            device_id_type=MESH,
        )
        copy.start()
        copies.append(copy)
    src[0:nblock] = feats_ref[...]
    table_ref[...] = slot_tables(cvec_ref[...], sends_ref, src.shape[0])
    fetch.wait()
    for copy in copies:
        copy.wait()

    def one_row(r, carry):
        lhs = jnp.concatenate([held[r, k] for k in range(ntile)], axis=1)
        rhs = jnp.concatenate([src[cols_ref[r, k]] for k in range(ntile)], axis=0)
        agg_ref[r] = jnp.dot(lhs, rhs, preferred_element_type=jnp.float32).astype(agg_ref.dtype)
        return carry

    swaps = []
    count = hsend.shape[0]
    for c in range(count):
        lax.fori_loop(c * nblock // count, (c + 1) * nblock // count, one_row, 0)
        span = pl.ds(c * nblock // count, nblock // count)
        swap = pltpu.make_async_remote_copy(
            src_ref=agg_ref.at[span],
            dst_ref=other_ref.at[span],
            send_sem=hsend.at[c],
            recv_sem=hrecv.at[c],
            device_id={"hid": peer},
            device_id_type=MESH,
        )
        swap.start()
        swaps.append(swap)
    for swap in swaps:
        swap.wait()


def front_call(tiles, cols, sends, blocks, shifts):
    nblock, _, width = blocks.shape
    nsend = sends.shape[2]
    return pl.pallas_call(
        functools.partial(front_kernel, shifts),
        in_specs=[SMEM_SPEC, VMEM_SPEC, SMEM_SPEC, VMEM_SPEC, ANY_SPEC],
        out_specs=[VMEM_SPEC] * 3,
        out_shape=[
            jax.ShapeDtypeStruct(blocks.shape, blocks.dtype),
            jax.ShapeDtypeStruct(blocks.shape, blocks.dtype),
            jax.ShapeDtypeStruct((8, LANES), jnp.int32),
        ],
        scratch_shapes=[
            VMEM(tiles.shape, tiles.dtype),
            VMEM((nblock + 3 * nsend, BLK, width), blocks.dtype),
            VMEM((3, nsend, BLK, width), blocks.dtype),
            pltpu.SemaphoreType.DMA,
            pltpu.SemaphoreType.DMA((3,)),
            pltpu.SemaphoreType.DMA((3,)),
            pltpu.SemaphoreType.DMA((4,)),
            pltpu.SemaphoreType.DMA((4,)),
        ],
        compiler_params=pltpu.CompilerParams(
            vmem_limit_bytes=56 << 20, collective_id=0, has_side_effects=True
        ),
        name="front",
    )(cols, cols, sends, blocks, tiles)


TRANS = (((1,), (1,)), ((), ()))
DEEP = (((0,), (0,)), ((), ()))


def rear_kernel(shifts, nbits, ntile, table, pins_ref, mine_ref, other_ref, w_ref, bias_ref, feats_ref, cotan_ref, tiles_ref, out_ref, dfeat_ref, dw_ref, db_ref, held, buf, dagg, dpre, dother, wx, b0, b1, b2, in0, in1, in2, wsum, outw, inw, gath, bsum, btmp, fetch_sem, xsend, xrecv, hsend, hrecv, bsend, brecv, rsend, rrecv, gsend, grecv, vsend, vrecv):
    nblock, _, width = dfeat_ref.shape
    rows = nblock * BLK
    ntiles = nblock * ntile
    slots = buf.shape[0] - 1
    nsend = b0.shape[0]
    high = gath.shape[0]
    me = lax.axis_index("dom")
    hid = lax.axis_index("hid")
    peer = 1 - hid
    fetch = pltpu.make_async_copy(tiles_ref, held.at[pl.ds(0, ntiles)], fetch_sem)
    fetch.start()
    greet([("dom", flipped(me, bit)) for bit in range(nbits)] + [("hid", peer)])

    def push(src, dst, send, recv, where):
        copy = pltpu.make_async_remote_copy(
            src_ref=src,
            dst_ref=dst,
            send_sem=send,
            recv_sem=recv,
            device_id=where,
            device_id_type=MESH,
        )
        copy.start()
        return copy

    def mate(bit):
        return {"dom": flipped(me, bit)}

    def wide(start, size):
        return pl.ds(pl.multiple_of(start, 16), size)

    here = wide(hid * width, width)
    there = wide(peer * width, width)
    wcopy = push(w_ref.at[there], wx, xsend, xrecv, {"hid": peer})
    wsum[...] = jnp.zeros_like(wsum)
    bsum[...] = jnp.zeros_like(bsum)
    chunk = 256

    def middle(i, carry):
        span = wide(i * chunk, chunk)
        mine, other = mine_ref[span, :], other_ref[span, :]
        pre = (
            jnp.dot(mine, w_ref[here, :], preferred_element_type=jnp.float32)
            + jnp.dot(other, w_ref[there, :], preferred_element_type=jnp.float32)
            + bias_ref[...]
        )
        ids = lax.broadcasted_iota(jnp.int32, (chunk, pins_ref.shape[1]), 0) + i * chunk
        hit = jnp.where(ids == pins_ref[...], 1.0, 0.0)
        keep = 1.0 - jnp.max(hit, axis=1, keepdims=True)
        sig = jax.nn.sigmoid(pre)
        out_ref[span, :] = (feats_ref[span, :].astype(jnp.float32) + keep * pre * sig).astype(
            out_ref.dtype
        )
        grad = (
            keep * cotan_ref[span, :].astype(jnp.float32) * sig * (1.0 + pre * (1.0 - sig))
        ).astype(dpre.dtype)
        dpre[span, :] = grad
        wsum[here, :] += lax.dot_general(mine, grad, DEEP, preferred_element_type=jnp.float32)
        wsum[there, :] += lax.dot_general(other, grad, DEEP, preferred_element_type=jnp.float32)
        bsum[...] += jnp.sum(grad.astype(jnp.float32).reshape(chunk // 8, 8, width), axis=0)
        return carry

    nchunk = hsend.shape[0]
    part = rows // nchunk
    swaps = []
    for c in range(nchunk):
        lax.fori_loop(c * part // chunk, (c + 1) * part // chunk, middle, 0)
        span = pl.ds(c * part, part)
        swaps.append(push(dpre.at[span], dother.at[span], hsend.at[c], hrecv.at[c], {"hid": peer}))

    state = {"start": me * 0, "size": high, "at": 0}

    def reduce_start(bit):
        half = state["size"] // 2
        upper = (me // (1 << bit)) % 2
        give = state["start"] + (1 - upper) * half
        state["start"] = state["start"] + upper * half
        state["size"] = half
        at = state["at"]
        outw[at : at + half] = wsum[wide(give, half)].astype(outw.dtype)
        outgoing = bsum if bit == 0 else btmp.at[2 * bit - 1]
        return (
            push(outw.at[pl.ds(at, half)], inw.at[pl.ds(at, half)], rsend.at[bit], rrecv.at[bit], mate(bit)),
            push(outgoing, btmp.at[2 * bit], vsend.at[bit], vrecv.at[bit], mate(bit)),
        )

    def reduce_end(bit, copies):
        for copy in copies:
            copy.wait()
        half, at = state["size"], state["at"]
        wsum[wide(state["start"], half)] += inw[at : at + half].astype(jnp.float32)
        outgoing = bsum[...] if bit == 0 else btmp[2 * bit - 1]
        btmp[2 * bit + 1] = outgoing + btmp[2 * bit]
        state["at"] = at + half
        if bit == nbits - 1:
            span = wide(state["start"], half)
            gath[span] = wsum[span].astype(gath.dtype)

    def gather_start(bit):
        span = wide(state["start"], state["size"])
        return (push(gath.at[span], gath.at[span], gsend.at[bit], grecv.at[bit], mate(bit)),)

    def gather_end(bit, copies):
        for copy in copies:
            copy.wait()
        state["start"] = state["start"] - ((me // (1 << bit)) % 2) * state["size"]
        state["size"] = state["size"] * 2

    stages = [(reduce_start, reduce_end, bit) for bit in range(nbits)]
    stages += [(gather_start, gather_end, bit) for bit in reversed(range(nbits))]

    flying = stages[0][0](stages[0][2])
    dagg[nblock] = jnp.zeros(dagg.shape[1:], dagg.dtype)
    held[ntiles] = jnp.zeros(held.shape[1:], held.dtype)
    buf[0] = jnp.zeros(buf.shape[1:], buf.dtype)
    for m, ref in enumerate((in0, in1, in2)):
        ref[nsend] = jnp.zeros(ref.shape[1:], ref.dtype)
    wcopy.wait()

    def undo(r, carry):
        span = wide(r * BLK, BLK)
        dagg[r] = (
            lax.dot_general(dpre[span, :], w_ref[here, :], TRANS, preferred_element_type=jnp.float32)
            + lax.dot_general(dother[span, :], wx[...], TRANS, preferred_element_type=jnp.float32)
        ).astype(dagg.dtype)
        return carry

    done = 0
    for c in range(nchunk):
        swaps[c].wait()
        lax.fori_loop(c * nblock // nchunk, (c + 1) * nblock // nchunk, undo, 0)
    fetch.wait()

    def one_slot(n, carry):
        lhs = jnp.concatenate([held[table[0, n * GROUP + g]] for g in range(GROUP)], axis=0)
        rhs = jnp.concatenate([dagg[table[1, n * GROUP + g]] for g in range(GROUP)], axis=0)
        prod = lax.dot_general(lhs, rhs, DEEP, preferred_element_type=jnp.float32)
        buf[n + 1] = buf[n] * table[3, n].astype(jnp.float32) + prod
        return carry

    nstage = len(stages) - done
    for i in range(nstage):
        lax.fori_loop(i * slots // nstage, (i + 1) * slots // nstage, one_slot, 0)
        stages[done + i][1](stages[done + i][2], flying)
        if i + 1 < nstage:
            flying = stages[done + i + 1][0](stages[done + i + 1][2])

    boxes = (b0, b1, b2)
    inboxes = (in0, in1, in2)
    backs = [None] * 3
    for m in (2, 1, 0):
        for j in range(nsend):
            boxes[m][j] = buf[table[2, nblock + m * nsend + j]].astype(b0.dtype)
        backs[m] = push(boxes[m], inboxes[m].at[pl.ds(0, nsend)], bsend.at[m], brecv.at[m], mate(shifts[m]))
    scale = 1.0 / math.sqrt((1 << nbits) * rows)
    dw_ref[...] = gath[...].astype(jnp.float32) * scale
    db_ref[...] = jnp.sum(btmp[2 * nbits - 1], axis=0, keepdims=True) * scale
    acc = []
    for m in range(3):
        backs[m].wait()
    for b in range(nblock):
        total = buf[table[2, b]] + cotan_ref[b * BLK : (b + 1) * BLK, :].astype(jnp.float32)
        for m in range(3):
            total = total + inboxes[m][table[4 + m, b]].astype(jnp.float32)
        dfeat_ref[b] = total.astype(dfeat_ref.dtype)


def rear_call(table, pins, mine, other, weight, bias, feats, cotan, tiles, nsend, shifts, nbits):
    rows, width = feats.shape
    nblock, ntile = tiles.shape[:2]
    ntiles = nblock * ntile
    high = weight.shape[0]
    slots = (ntiles + (GROUP - 1) * (nblock + 3 * nsend)) // GROUP
    sem = pltpu.SemaphoreType.DMA
    half = feats.dtype
    return pl.pallas_call(
        functools.partial(rear_kernel, shifts, nbits, ntile),
        in_specs=[SMEM_SPEC] + [VMEM_SPEC] * 7 + [ANY_SPEC],
        out_specs=[VMEM_SPEC] * 4,
        out_shape=[
            jax.ShapeDtypeStruct((rows, width), half),
            jax.ShapeDtypeStruct((nblock, BLK, width), half),
            jax.ShapeDtypeStruct((high, width), jnp.float32),
            jax.ShapeDtypeStruct((1, width), jnp.float32),
        ],
        scratch_shapes=[
            VMEM((ntiles + 1, BLK, BLK), half),
            VMEM((slots + 1, BLK, width), jnp.float32),
            VMEM((nblock + 1, BLK, width), half),
            VMEM((rows, width), half),
            VMEM((rows, width), half),
            VMEM((width, width), half),
        ]
        + [VMEM((nsend, BLK, width), half)] * 3
        + [VMEM((nsend + 1, BLK, width), half)] * 3
        + [VMEM((high, width), jnp.float32)]
        + [VMEM((high, width), half)] * 3
        + [
            VMEM((8, width), jnp.float32),
            VMEM((2 * nbits, 8, width), jnp.float32),
            sem,
            sem,
            sem,
            sem((4,)),
            sem((4,)),
            sem((3,)),
            sem((3,)),
        ]
        + [sem((nbits,))] * 6,
        compiler_params=pltpu.CompilerParams(
            vmem_limit_bytes=60 << 20, collective_id=1, has_side_effects=True
        ),
        name="rear",
    )(
        table,
        pins,
        mine,
        other,
        weight,
        bias.reshape(1, width),
        feats,
        cotan,
        tiles.reshape(ntiles, BLK, BLK),
    )


def emit_kernel(count, *refs):
    given, taken, held = refs[:count], refs[count : 2 * count], refs[2 * count : 3 * count]
    sems = refs[-1]
    reads = [pltpu.make_async_copy(given[i], held[i], sems.at[0, i]) for i in range(count)]
    writes = [pltpu.make_async_copy(held[i], taken[i], sems.at[1, i]) for i in range(count)]
    for read in reads:
        read.start()
    for read, write in zip(reads, writes):
        read.wait()
        write.start()
    for write in writes:
        write.wait()


def emit_call(*arrays):
    count = len(arrays)
    return pl.pallas_call(
        functools.partial(emit_kernel, count),
        in_specs=[ANY_SPEC] * count,
        out_specs=[ANY_SPEC] * count,
        out_shape=[jax.ShapeDtypeStruct(one.shape, one.dtype) for one in arrays],
        scratch_shapes=[VMEM(one.shape, one.dtype) for one in arrays]
        + [pltpu.SemaphoreType.DMA((2, count))],
        compiler_params=pltpu.CompilerParams(vmem_limit_bytes=56 << 20),
        name="emit",
    )(*arrays)


def body(feats, tiles, tile_cols, sends, pins, weight, bias, cotan):
    rows, width = feats.shape
    nblock = rows // BLK
    nsend = sends.shape[2]
    nbits = lax.axis_size("dom").bit_length() - 1
    shifts = (0, nbits // 2, nbits - 1)
    blocks = feats.reshape(nblock, BLK, width)
    agg, other, table = front_call(tiles, tile_cols, sends, blocks, shifts)
    agg, other = agg.reshape(rows, width), other.reshape(rows, width)
    out, dfeat, dweight, dbias = rear_call(
        table, pins, agg, other, weight, bias, feats, cotan, tiles, nsend, shifts, nbits
    )
    out, dfeat, dweight, dbias = emit_call(out, dfeat, dweight, dbias)
    return (out, dfeat.reshape(rows, width), dweight, dbias.reshape(-1))


def solution(mesh):
    return jax.shard_map(
        body,
        mesh=mesh,
        in_specs=(
            P(("basin", "dom"), "hid"),
            P(("basin", "dom"), None, None, None),
            P(("basin", "dom"), None),
            P(("basin", "dom"), None, None),
            P(("basin", "dom"), None),
            P(None, "hid"),
            P("hid"),
            P(("basin", "dom"), "hid"),
        ),
        out_specs=(
            P(("basin", "dom"), "hid"),
            P(("basin", "dom"), "hid"),
            P("basin", "hid"),
            P(("basin", "hid")),
        ),
        check_vma=False,
    )
```
